32 devices in a mesh: spec: 4 (over y, core), wave: 8 (over z, x).
Axes of the slice: x: 2, y: 2, z: 4, core: 2. Of those that a mesh axis runs over, the one named last changes fastest.
Arguments:
- templates: float32 [48, 10, 4096], P('spec', None, 'wave'), as said below
- resolution: float32 [256, 11, 4096], P('spec', None, 'wave'), may hold values from 0.02 to 0.2
- coadd_flux: float32 [256, 4096], P('spec', 'wave'), as said below
- coadd_ivar: float32 [256, 4096], P('spec', 'wave'), may hold values from 0.1 to 2
- best_index: int32 [256], P('spec'), may hold values from 0 to 47, as said below
- exposures: float32 [256, 3, 4096], P(('spec', 'wave')), may hold values from -6 to 6
- exposure_mask: int32 [256, 3, 4096], P(('spec', 'wave')), may hold values 0 or 1
Outputs:
- fit_gain: float32 [256, 48], P(('spec', 'wave'))
- residuals: float32 [256, 3, 4096], P(('spec', 'wave'))
The draws below stay inside these ranges and needn't reach their ends.
Inputs may be any that keep to these rules, and one draw needn't show every extreme that they name: Redshifted templates, one set of 10 for each of the 48 redshifts. `coadd_flux`: coadded flux of each spectrum. `best_index`: an index into the 48 redshifts.
All inputs are finite; a program needn't handle non-finite values. No bound on the sum of `exposure_mask` on one device may be relied on, other than what follows from the above.
Results may differ from the reference program's by a relative error of at most 0.000073.
Values sent between devices are 32-bit elements; how exact they have to be, the bound alone decides.
No kernel may reach another device: no remote copies, remote signals or barrier semaphores. Data moves between devices by JAX's collectives and lax.ppermute only.
A program may use at most 192 MiB of HBM per device.

```python
import math
import jax
import jax.numpy as jnp
from jax import lax

NT = 10
BAND = 11
NEXP = 3
SPECTRA = 256
REDSHIFTS = 48
PIXELS = 4096


def common_draw(key):
    first_key = jax.random.fold_in(key, 101)
    second_key = jax.random.fold_in(key, 102)
    third_key = jax.random.fold_in(key, 103)
    fourth_key = jax.random.fold_in(key, 104)
    fifth_key = jax.random.fold_in(key, 105)
    private = jax.random.normal(first_key, (REDSHIFTS, NT, PIXELS), jnp.float32)
    shared = jax.random.normal(second_key, (REDSHIFTS, 1, PIXELS), jnp.float32)
    templates = private + 0.7 * shared
    chosen = jax.random.randint(third_key, (SPECTRA,), 0, REDSHIFTS)
    chosen = chosen.at[0].set(REDSHIFTS - 1).at[1].set(0)
    amounts = 0.5 * jax.random.normal(fourth_key, (SPECTRA, NT), jnp.float32)
    scatter_noise = jax.random.normal(fifth_key, (SPECTRA, PIXELS), jnp.float32)
    return (templates, chosen, amounts, scatter_noise)


def draw_templates(key, part):
    return common_draw(key)[0]


def draw_best_index(key, part):
    return common_draw(key)[1].astype(jnp.int32)


def draw_coadd_flux(key, part):
    templates, chosen, amounts, scatter_noise = common_draw(key)
    signal = jnp.zeros((SPECTRA, PIXELS), jnp.float32)
    for template_number in range(NT):
        signal = signal + amounts[:, template_number, None] * templates[chosen, template_number, :]
    return signal + scatter_noise


def set_ends(array, stream_key, least, largest):
    longest = array.shape.index(max(array.shape))
    spots = []
    for shift in (0, 1):
        where = [jax.random.randint(jax.random.fold_in(stream_key, axis), (), 0, length) for axis, length in enumerate(array.shape)]
        where[longest] = (where[longest] + shift) % array.shape[longest]
        spots.append(tuple(where))
    return array.at[spots[0]].set(least).at[spots[1]].set(largest)


def block_scale(rng, dims, cuts, smallest, largest):
    gain, own = 1.0, jax.random.fold_in(rng, 6)
    for dim, shards_of in cuts:
        draws = jnp.exp(jax.random.uniform(jax.random.fold_in(own, dim), (shards_of,), jnp.float32, smallest / len(cuts), largest / len(cuts)))
        gain = gain * jnp.repeat(draws, dims[dim] // shards_of).reshape([-1 if axis == dim else 1 for axis in range(len(dims))])
    return gain


def normal_values(rng, shape, spread, bound, split=(), dtype=jnp.bfloat16):
    level = block_scale(rng, shape, split, -0.22, 0.18) if split else 1.0
    values = jax.random.normal(rng, shape, jnp.float32) * spread * level
    return jnp.minimum(jnp.maximum(values, -bound), bound).astype(dtype)


def setup_inputs(seed: int = 0) -> dict:
    keys = jax.random.split(jax.random.key(seed), 8)
    return {
        "templates": draw_templates(jax.random.fold_in(keys[7], 71), 0),
        "resolution": jnp.clip(0.02 + 0.18 * jax.random.uniform(keys[1], (SPECTRA, BAND, PIXELS), jnp.float32) ** block_scale(keys[1], (SPECTRA, BAND, PIXELS), ((0, 4), (2, 8)), -0.2, 0.2), 0.02, 0.2),
        "coadd_flux": draw_coadd_flux(jax.random.fold_in(keys[7], 71), 0),
        "coadd_ivar": jnp.clip(jnp.exp(math.log(2.0) - 2.9957323 * jax.random.uniform(keys[3], (SPECTRA, PIXELS), jnp.float32) ** block_scale(keys[3], (SPECTRA, PIXELS), ((0, 4), (1, 8)), -0.2, 0.2)), 0.1, 2.0),
        "best_index": draw_best_index(jax.random.fold_in(keys[7], 71), 0),
        "exposures": normal_values(keys[5], (SPECTRA, NEXP, PIXELS), 1.0, 6.0, ((0, 32),), jnp.float32),
        "exposure_mask": set_ends((jax.random.randint(keys[6], (SPECTRA, NEXP, PIXELS), 0, 5) < 4).astype(jnp.int32), jax.random.fold_in(keys[6], 1), 0, 1),
    }


def band_apply(band_rows, source, pixel_count):
    accumulated = band_rows[0] * source[..., 0:pixel_count]
    for offset in range(1, band_rows.shape[0]):
        accumulated = accumulated + band_rows[offset] * source[..., offset:offset + pixel_count]
    return accumulated

def reference(templates, resolution, coadd_flux, coadd_ivar, best_index, exposures, exposure_mask):
    half_band = BAND // 2
    padded = jnp.pad(templates, ((0, 0), (0, 0), (half_band, half_band)))
    weight_root = jnp.sqrt(coadd_ivar)
    target = coadd_flux * weight_root

    def one_spectrum(spectrum_items):
        band_rows, root_row, target_row, chosen = spectrum_items
        weighted_basis = band_apply(band_rows * root_row[None, :], padded, PIXELS)
        normal = jnp.einsum('zkp,zlp->zkl', weighted_basis, weighted_basis, precision=lax.Precision.HIGHEST)
        projection = jnp.einsum('zkp,p->zk', weighted_basis, target_row, precision=lax.Precision.HIGHEST)
        factor = jnp.linalg.cholesky(normal)
        coefficients = jax.scipy.linalg.cho_solve((factor, True), projection[..., None])[..., 0]
        fit_row = jnp.log1p(lax.optimization_barrier(jnp.sum(projection * coefficients, axis=1)) / NT)
        chosen_source = lax.dynamic_index_in_dim(padded, chosen, 0, keepdims=False)
        best_basis = band_apply(band_rows, chosen_source, PIXELS)
        best_coef = lax.dynamic_index_in_dim(coefficients, chosen, 0, keepdims=False)
        model_row = jnp.einsum('k,kp->p', best_coef, best_basis, precision=lax.Precision.HIGHEST)
        return (fit_row, model_row)
    fit_gain, model_rows = lax.map(one_spectrum, (resolution, weight_root, target, best_index))
    residuals = exposure_mask.astype(jnp.float32) * (exposures - model_rows[:, None, :])
    return (fit_gain, residuals)
```

```python
import jax
import jax.numpy as jnp
from jax import lax
from jax.experimental import pallas as pl
from jax.experimental.pallas import tpu as pltpu
from jax.sharding import PartitionSpec as P

LANES = 128
BF = jnp.bfloat16

def split(x):
    hi = x.astype(BF)
    lo = (x - hi.astype(jnp.float32)).astype(BF)
    return hi, lo

def band_matrix(r_ref, flux_ref, ivar_ref, wb_ref, a_ref, ae_ref):
    band, S, W = r_ref.shape
    half = band // 2
    wide = W + LANES
    root = jnp.sqrt(ivar_ref[...])
    for d in range(band):
        wb_ref[d] = r_ref[d] * root
    wb_ref[band] = flux_ref[...] * root
    R = 16
    lane = lax.broadcasted_iota(jnp.int32, (R, LANES), 1)
    zero = jnp.zeros((R, LANES), jnp.float32)
    for c in range(S // R):
        rows = pl.ds(c * R, R)
        edge = zero
        for delta in range(band + 1):
            total = None
            taps = range(band - delta) if delta < band else range(band)
            for d in taps:
                other = d + delta if delta < band else band
                term = wb_ref[d, rows, :] * wb_ref[other, rows, :]
                term = jnp.concatenate([term, zero], axis=1)
                shift = (d - half) % wide
                if shift:
                    term = pltpu.roll(term, shift, 1)
                total = term if total is None else total + term
            if delta == 0:
                total = total * 0.5
            hi, lo = split(total[:, :W])
            a_ref[delta, pl.ds(c * R, R), :] = jnp.concatenate([hi, hi], axis=1)
            a_ref[delta, pl.ds(S + c * R, R), :] = jnp.concatenate([lo, lo], axis=1)
            base = 2 * half * delta if delta < band else 0
            back = delta if delta < band else 0
            left = pltpu.roll(total, (base + half) % wide, 1)[:, :LANES]
            right = pltpu.roll(total, (base + half - (W - back)) % wide, 1)[:, :LANES]
            prev = edge if delta < band else zero
            new = jnp.where((lane >= base) & (lane < base + half), left,
                   jnp.where((lane >= base + half) & (lane < base + 2 * half), right, prev))
            if delta < band:
                edge = new
                if delta == band - 1:
                    slot, val = 0, edge
            if delta == band:
                slot, val = 1, new
            if delta >= band - 1:
                hi, lo = split(val)
                ae_ref[slot, pl.ds(c * R, R), :] = hi
                ae_ref[slot, pl.ds(S + c * R, R), :] = lo

def nt(x, w):
    return lax.dot_general(x, w, (((1,), (1,)), ((), ())), preferred_element_type=jnp.float32)

def make_main(K, Z, band, S, W, overlap=True):
    pairs = [(k, l) for k in range(K) for l in range(k, K)]
    NP = len(pairs)
    ZB = 16
    nb = Z // ZB
    half = band // 2
    wide = W + LANES

    def kernel(t_ref, x_ref, r_ref, flux_ref, ivar_ref, out_ref,
               wb_ref, a_ref, ae_ref, s_ref, h_ref, acc_ref):
        band_matrix(r_ref, flux_ref, ivar_ref, wb_ref, a_ref, ae_ref)
        acc_ref[...] = jnp.zeros_like(acc_ref)
        s_ref[:, :, :W] = t_ref[...]
        s_ref[:, :, W:] = jnp.zeros((K, Z, LANES), jnp.float32)

        def build(b, first):
            rows = pl.ds(b * ZB, ZB)
            for q in range(W // LANES):
                lanes = pl.ds(q * LANES, LANES)
                t = [t_ref[k, rows, lanes] for k in range(K)]
                s = [s_ref[k, rows, lanes] for k in range(K)]
                for i, (k, l) in enumerate(pairs):
                    h = t[k] * s[l] + t[l] * s[k]
                    hi, lo = split(h)
                    h_ref[i, rows, lanes] = hi
                    h_ref[i, rows, pl.ds(W + q * LANES, LANES)] = lo

        def shift_s():
            for k in range(K):
                for b in range(Z // 8):
                    rows = pl.ds(b * 8, 8)
                    s_ref[k, rows, :] = pltpu.roll(s_ref[k, rows, :], wide - 1, 1)

        def step(delta, _):
            for b in range(nb):
                build(b, False)
                rows = pl.ds(b * ZB, ZB)
                hb = h_ref[:, rows, :].reshape(NP * ZB, 2 * W)
                acc_ref[:NP, rows, :] += nt(hb, a_ref[delta]).reshape(NP, ZB, 2 * S)
            shift_s()
            return 0
        lax.fori_loop(0, band, step, 0)
        for b in range(nb):
            rows = pl.ds(b * ZB, ZB)
            for k in range(K):
                hi, lo = split(t_ref[k, rows, :])
                h_ref[k, rows, :W] = hi
                h_ref[k, rows, W:] = lo
        hb = h_ref[:K].reshape(K * Z, 2 * W)
        acc_ref[NP:] += nt(hb, a_ref[band]).reshape(K, Z, 2 * S)
        inp = lax.broadcasted_iota(jnp.int32, (LANES, LANES), 0)
        outp = lax.broadcasted_iota(jnp.int32, (LANES, LANES), 1)
        dd = outp // (2 * half)
        ii = outp % (2 * half)
        isl = ii < half
        valid = outp < 2 * half * band
        src1 = jnp.where(isl, ii, 64 + half + ii)
        src2 = jnp.where(isl, ii + dd, 64 + half + ii - dd)
        sel1 = ((inp == src1) & valid).astype(jnp.float32)
        sel2 = ((inp == src2) & valid).astype(jnp.float32)
        x = x_ref[...].reshape(K * Z, LANES)
        hp = lax.Precision.HIGHEST
        e1 = jnp.dot(x, sel1, precision=hp, preferred_element_type=jnp.float32).reshape(K, Z, LANES)
        e2 = jnp.dot(x, sel2, precision=hp, preferred_element_type=jnp.float32).reshape(K, Z, LANES)
        s_ref[:, :, :LANES] = e1
        s_ref[:, :, LANES:2 * LANES] = e2
        for b in range(nb):
            rows = pl.ds(b * ZB, ZB)
            t = [s_ref[k, rows, :LANES] for k in range(K)]
            s = [s_ref[k, rows, LANES:2 * LANES] for k in range(K)]
            for i, (k, l) in enumerate(pairs):
                hi, lo = split(t[k] * s[l] + t[l] * s[k])
                h_ref[i, rows, :LANES] = hi
                h_ref[i, rows, LANES:2 * LANES] = lo
        w = jnp.concatenate([ae_ref[0], ae_ref[0]], axis=1)
        acc_ref[:NP] += nt(h_ref[:NP, :, :2 * LANES].reshape(NP * Z, 2 * LANES), w).reshape(NP, Z, 2 * S)
        for b in range(nb):
            rows = pl.ds(b * ZB, ZB)
            for k in range(K):
                hi, lo = split(s_ref[k, rows, :LANES])
                h_ref[k, rows, :LANES] = hi
                h_ref[k, rows, LANES:2 * LANES] = lo
        w = jnp.concatenate([ae_ref[1], ae_ref[1]], axis=1)
        acc_ref[NP:] += nt(h_ref[:K, :, :2 * LANES].reshape(K * Z, 2 * LANES), w).reshape(K, Z, 2 * S)
        full = acc_ref[...].reshape((NP + K) * Z, 2 * S).T
        out_ref[...] = full[:S] + full[S:]

    n = (NP + K) * Z
    return pl.pallas_call(kernel, out_shape=jax.ShapeDtypeStruct((S, n), jnp.float32),
        scratch_shapes=[pltpu.VMEM((band + 1, S, W), jnp.float32),
                        pltpu.VMEM((band + 1, 2 * S, 2 * W), BF),
                        pltpu.VMEM((2, 2 * S, LANES), BF),
                        pltpu.VMEM((K, Z, wide), jnp.float32),
                        pltpu.VMEM((NP, Z, 2 * W), BF),
                        pltpu.VMEM((NP + K, Z, 2 * S), jnp.float32)],
        compiler_params=pltpu.CompilerParams(vmem_limit_bytes=60 << 20),
        name="normals")


def solve_kernel_for(K, Z, pairs):
    NP = len(pairs)

    def kernel(parts_ref, best_ref, gain_ref, coef_ref):
        n = jnp.sum(parts_ref[...], axis=0)

        def item(i):
            return n[:, i * Z:(i + 1) * Z]
        N = {kl: item(i) for i, kl in enumerate(pairs)}
        proj = [item(NP + k) for k in range(K)]
        L, inv, y = {}, [], []
        for j in range(K):
            for i in range(j, K):
                v = N[(j, i)]
                for m in range(j):
                    v = v - L[(i, m)] * L[(j, m)]
                L[(i, j)] = v
            root = jnp.sqrt(L[(j, j)])
            inv.append(1.0 / root)
            for i in range(j + 1, K):
                L[(i, j)] = L[(i, j)] * inv[j]
            v = proj[j]
            for m in range(j):
                v = v - L[(j, m)] * y[m]
            y.append(v * inv[j])
        c = [None] * K
        for j in reversed(range(K)):
            v = y[j]
            for i in range(j + 1, K):
                v = v - L[(i, j)] * c[i]
            c[j] = v * inv[j]
        chi = proj[0] * c[0]
        for k in range(1, K):
            chi = chi + proj[k] * c[k]
        gain_ref[...] = jnp.log1p(chi / K)
        rows = n.shape[0]
        hit = lax.broadcasted_iota(jnp.int32, (rows, Z), 1) == best_ref[...]
        lane = lax.broadcasted_iota(jnp.int32, (rows, LANES), 1)
        out = jnp.zeros((rows, LANES), jnp.float32)
        for k in range(K):
            v = jnp.sum(jnp.where(hit, c[k], 0.0), axis=1, keepdims=True)
            out = jnp.where(lane == k, v, out)
        coef_ref[...] = out
    return kernel


def model_kernel_for(K, Z, band):
    half = band // 2
    hp = lax.Precision.HIGHEST

    def kernel(t_ref, x_ref, r_ref, coef_ref, best_ref, out_ref):
        S, W = out_ref.shape
        hit = lax.broadcasted_iota(jnp.int32, (S, Z), 1) == best_ref[...]
        main = jnp.zeros((S, W), jnp.float32)
        edge = jnp.zeros((S, LANES), jnp.float32)
        for k in range(K):
            sel = jnp.where(hit, coef_ref[:, k:k + 1], 0.0)
            main = main + jnp.dot(sel, t_ref[k], precision=hp, preferred_element_type=jnp.float32)
            edge = edge + jnp.dot(sel, x_ref[k], precision=hp, preferred_element_type=jnp.float32)
        lane = lax.broadcasted_iota(jnp.int32, (S, LANES), 1)
        right = pltpu.roll(edge, LANES - (64 + 2 * half), 1)
        left = pltpu.roll(edge, LANES - half, 1)
        last = jnp.where(lane < half, right, jnp.where(lane >= LANES - half, left, 0.0))
        u = jnp.concatenate([main, last], axis=1)
        wide = W + LANES
        total = None
        for d in range(band):
            shift = (half - d) % wide
            v = (pltpu.roll(u, shift, 1) if shift else u)[:, :W]
            term = r_ref[d] * v
            total = term if total is None else total + term
        out_ref[...] = total
    return kernel


def body(templates, resolution, coadd_flux, coadd_ivar, best_index, exposures, exposure_mask):
    S, band, W = resolution.shape
    half = band // 2
    K = templates.shape[1]
    nw, ns = lax.axis_size("wave"), lax.axis_size("spec")
    Z = templates.shape[0] * ns
    own = S // nw
    pairs = [(k, l) for k in range(K) for l in range(k, K)]
    columns = (len(pairs) + K) * Z
    up = [(i, i + 1) for i in range(nw - 1)]
    down = [(j, i) for i, j in up]
    before = lax.ppermute(templates[:, :, W - half:], "wave", up)
    after = lax.ppermute(templates[:, :, :half], "wave", down)
    padded = jnp.concatenate([before, templates, after], axis=2)
    full = lax.all_gather(padded, "spec", axis=0, tiled=True)
    full = jnp.transpose(full, (1, 0, 2))
    t = full[:, :, half:half + W]
    x = jnp.concatenate([full[:, :, :3 * half], jnp.zeros((K, Z, 64 - 3 * half), jnp.float32),
                         full[:, :, W - half:], jnp.zeros((K, Z, 64 - 3 * half), jnp.float32)], axis=2)
    r = jnp.transpose(resolution, (1, 0, 2))
    partial = make_main(K, Z, band, S, W)(t, x, r, coadd_flux, coadd_ivar)
    parts = lax.all_to_all(partial.reshape(nw, own, columns), "wave", 0, 0, tiled=True)
    own_best = lax.dynamic_slice_in_dim(best_index, lax.axis_index("wave") * own, own)
    gain, coef = pl.pallas_call(
        solve_kernel_for(K, Z, pairs),
        out_shape=(jax.ShapeDtypeStruct((own, Z), jnp.float32),
                   jax.ShapeDtypeStruct((own, LANES), jnp.float32)),
        name="solve",
    )(parts, own_best[:, None])
    spread = jnp.broadcast_to(coef[None], (nw, own, LANES))
    coefs = lax.all_to_all(spread, "wave", 0, 0, tiled=True).reshape(S, LANES)
    model = pl.pallas_call(
        model_kernel_for(K, Z, band),
        out_shape=jax.ShapeDtypeStruct((S, W), jnp.float32),
        name="model",
    )(t, x, r, coefs, best_index[:, None])
    rows = lax.all_to_all(model.reshape(nw, own, W), "wave", 0, 0, tiled=True)
    rows = jnp.transpose(rows, (1, 0, 2)).reshape(own, 1, nw * W)
    residuals = exposure_mask.astype(jnp.float32) * (exposures - rows)
    return gain, residuals


def solution(mesh):
    in_specs = (
        P("spec", None, "wave"),
        P("spec", None, "wave"),
        P("spec", "wave"),
        P("spec", "wave"),
        P("spec"),
        P(("spec", "wave"), None, None),
        P(("spec", "wave"), None, None),
    )
    out_specs = (P(("spec", "wave"), None), P(("spec", "wave"), None, None))
    return jax.shard_map(body, mesh=mesh, in_specs=in_specs, out_specs=out_specs, check_vma=False)
```

```python
import jax
import jax.numpy as jnp
from jax import lax
from jax.experimental import pallas as pl
from jax.experimental.pallas import tpu as pltpu
from jax.sharding import PartitionSpec as P


LANES = 128
BF = jnp.bfloat16


def split(x):
    hi = x.astype(BF)
    return hi, (x - hi.astype(jnp.float32)).astype(BF)


def dot(x, w):
    return jnp.dot(x, w, preferred_element_type=jnp.float32)


def pair_list(K):
    return [(k, l) for k in range(K) for l in range(k, K)]


def put(h_ref, row, q, width, a, c):
    hi, lo = split(jnp.concatenate([a, c], axis=0))
    h_ref[row, :, q * LANES:(q + 1) * LANES] = hi
    h_ref[row, :, width + q * LANES:width + (q + 1) * LANES] = lo


def pair_block(h_ref, t, s, b, blocks, q, width):
    pairs = pair_list(len(t))
    items = [t[k] * s[l] + t[l] * s[k] for k, l in pairs]
    items += [jnp.zeros_like(t[0])] * (len(pairs) % 2)
    for i in range(len(items) // 2):
        put(h_ref, i * blocks + b, q, width, items[2 * i], items[2 * i + 1])


def single_block(h_ref, t, b, blocks, q, width):
    items = t + [jnp.zeros_like(t[0])] * (len(t) % 2)
    for i in range(len(items) // 2):
        put(h_ref, i * blocks + b, q, width, items[2 * i], items[2 * i + 1])


def make_main(K, Z, band, S, W):
    pairs = pair_list(K)
    NP = len(pairs)
    NQ = (NP + 1) // 2
    KQ = (K + 1) // 2
    ZB = Z // 8
    half = band // 2
    wide = W + LANES
    top = 24
    N = 2 * S
    step = 16

    def band_matrix(own_ref, other_ref, wb_ref, a_ref, rhs_ref, edge_ref, aeb_ref):
        root_own = jnp.sqrt(own_ref[band])
        root_other = jnp.sqrt(other_ref[band])
        zero = jnp.zeros((band + 1, top, N), jnp.float32)
        wb_ref[:, :top, :] = zero
        wb_ref[:, top + W:, :] = zero
        for d in range(band + 1):
            src = d if d < band else band + 1
            both = jnp.concatenate([own_ref[src] * root_own, other_ref[src] * root_other], axis=0)
            wb_ref[d, top:top + W, :] = both.T

        def block(i, _):
            base = pl.multiple_of(i * step, step)
            for part in range(step // 8):
                acc = [None] * (band + 1)
                for d in range(band):
                    rows = pl.ds(base + (part * 8 + top - step + half - d), 8)
                    v = [wb_ref[e, rows, :] for e in range(d, band + 1)]
                    for e in range(d, band + 1):
                        o = e - d if e < band else band
                        p = v[0] * v[e - d]
                        acc[o] = p if acc[o] is None else acc[o] + p
                acc[0] = acc[0] * 0.5
                for o in range(band + 1):
                    a_ref[o, pl.ds(base + part * 8, 8), :] = acc[o]
            for o in range(band + 1):
                hi, lo = split(a_ref[o, pl.ds(base, step), :])
                rhs_ref[o, pl.ds(base, step), :N] = hi
                rhs_ref[o, pl.ds(base, step), N:] = lo
            return 0

        lax.fori_loop(0, (W + 2 * step) // step, block, 0)
        edge_ref[...] = jnp.zeros_like(edge_ref)
        for o in range(band):
            edge_ref[0, 2 * half * o:2 * half * o + half, :] = a_ref[o, step - half:step, :]
            edge_ref[0, 2 * half * o + half:2 * half * (o + 1), :] = a_ref[o, step + W - o:step + W - o + half, :]
        edge_ref[1, :half, :] = a_ref[band, step - half:step, :]
        edge_ref[1, half:2 * half, :] = a_ref[band, step + W:step + W + half, :]
        for o in range(2):
            hi, lo = split(edge_ref[o])
            aeb_ref[o, :, :N] = hi
            aeb_ref[o, :, N:] = lo

    def kernel(t_ref, own_ref, other_ref, out_ref, aeb_ref,
               wb_ref, a_ref, rhs_ref, edge_ref, s_ref, h0_ref, h1_ref, acc_ref):
        band_matrix(own_ref, other_ref, wb_ref, a_ref, rhs_ref, edge_ref, aeb_ref)
        s_ref[:, :, :W] = t_ref[...]
        s_ref[:, :, W:] = jnp.zeros((K, Z, LANES), jnp.float32)
        acc_ref[...] = jnp.zeros_like(acc_ref)

        def build(h_ref):
            for b in range(ZB):
                rows = pl.ds(b * 8, 8)
                for q in range(W // LANES):
                    lanes = pl.ds(q * LANES, LANES)
                    t = [t_ref[k, rows, lanes] for k in range(K)]
                    s = [s_ref[k, rows, lanes] for k in range(K)]
                    pair_block(h_ref, t, s, b, ZB, q, W)

        def advance():
            for k in range(K):
                for b in range(ZB):
                    rows = pl.ds(b * 8, 8)
                    s_ref[k, rows, :] = pltpu.roll(s_ref[k, rows, :], wide - 1, 1)

        def add(h_ref, first, count, width, w):
            h = h_ref[:count, :, :2 * width].reshape(count * 16, 2 * width)
            v = dot(h[:, :width], w) + dot(h[:, width:], w)
            acc_ref[first:first + count] += v.reshape(count, 16, 2 * N)

        def weights(o):
            return rhs_ref[o, step:step + W, :]

        build(h0_ref)
        advance()

        def pair_step(i, _):
            build(h1_ref)
            advance()
            add(h0_ref, 0, NQ * ZB, W, weights(2 * i))
            build(h0_ref)
            advance()
            add(h1_ref, 0, NQ * ZB, W, weights(2 * i + 1))
            return 0

        lax.fori_loop(0, band // 2, pair_step, 0)
        for b in range(ZB):
            rows = pl.ds(b * 8, 8)
            for q in range(W // LANES):
                single_block(h1_ref, [t_ref[k, rows, pl.ds(q * LANES, LANES)] for k in range(K)], b, ZB, q, W)
        add(h0_ref, 0, NQ * ZB, W, weights(band - 1))
        add(h1_ref, NQ * ZB, KQ * ZB, W, weights(band))
        acc = acc_ref[:, :, :N] + acc_ref[:, :, N:]
        out_ref[...] = acc.reshape((NQ + KQ) * ZB * 16, N)

    return pl.pallas_call(
        kernel,
        out_shape=(jax.ShapeDtypeStruct(((NQ + KQ) * ZB * 16, N), jnp.float32),
                   jax.ShapeDtypeStruct((2, LANES, 2 * N), BF)),
        scratch_shapes=[pltpu.VMEM((band + 1, W + 2 * top, N), jnp.float32),
                        pltpu.VMEM((band + 1, W + 2 * step, N), jnp.float32),
                        pltpu.VMEM((band + 1, W + 2 * step, 2 * N), BF),
                        pltpu.VMEM((2, LANES, N), jnp.float32),
                        pltpu.VMEM((K, Z, wide), jnp.float32),
                        pltpu.VMEM((NQ * ZB, 16, 2 * W), BF),
                        pltpu.VMEM((NQ * ZB, 16, 2 * W), BF),
                        pltpu.VMEM(((NQ + KQ) * ZB, 16, 2 * N), jnp.float32)],
        compiler_params=pltpu.CompilerParams(vmem_limit_bytes=60 << 20),
        name="normals")


def make_edge(K, Z, band, S, planes, own):
    NP = K * (K + 1) // 2
    NQ, KQ, ZB = (NP + 1) // 2, (K + 1) // 2, Z // 8
    half = band // 2
    N = 2 * S
    hp = lax.Precision.HIGHEST

    def kernel(acc_ref, aeb_ref, x_ref, own_ref, other_ref, out_ref, nb_ref, nb2_ref, h_ref):
        inp = lax.broadcasted_iota(jnp.int32, (LANES, LANES), 0)
        outp = lax.broadcasted_iota(jnp.int32, (LANES, LANES), 1)
        dd = outp // (2 * half)
        ii = outp % (2 * half)
        isl = ii < half
        valid = outp < 2 * half * band
        src1 = jnp.where(isl, ii, 64 + half + ii)
        src2 = jnp.where(isl, ii + dd, 64 + half + ii - dd)
        sel1 = ((inp == src1) & valid).astype(jnp.float32)
        sel2 = ((inp == src2) & valid).astype(jnp.float32)
        x = x_ref[...].reshape(K * Z, LANES)
        e1 = jnp.dot(x, sel1, precision=hp, preferred_element_type=jnp.float32).reshape(K, Z, LANES)
        e2 = jnp.dot(x, sel2, precision=hp, preferred_element_type=jnp.float32).reshape(K, Z, LANES)
        for b in range(ZB):
            t = [e1[k, b * 8:(b + 1) * 8] for k in range(K)]
            s = [e2[k, b * 8:(b + 1) * 8] for k in range(K)]
            pair_block(h_ref, t, s, b, ZB, 0, LANES)
            single_block(h_ref.at[NQ * ZB:], t, b, ZB, 0, LANES)
        h = h_ref[...].reshape((NQ + KQ) * ZB * 16, 2 * LANES)
        cut = NQ * ZB * 16
        sums = []
        for part, o in ((h[:cut], 0), (h[cut:], 1)):
            v = dot(part[:, :LANES], aeb_ref[o]) + dot(part[:, LANES:], aeb_ref[o])
            sums.append(v[:, :N] + v[:, N:])
        acc = acc_ref[...] + jnp.concatenate(sums, axis=0)
        acc = acc.reshape(NQ + KQ, ZB, 2, 8, N)
        place = jnp.concatenate([own_ref[0], other_ref[0]], axis=0).T[:1, :]
        zrow = lax.broadcasted_iota(jnp.int32, (Z, N), 0).astype(jnp.float32)
        hit = zrow == place
        nb_ref[...] = jnp.zeros_like(nb_ref)
        nb2_ref[...] = jnp.zeros_like(nb2_ref)
        parts = []
        for n in range(NP + K):
            i, par = (n // 2, n % 2) if n < NP else (NQ + (n - NP) // 2, (n - NP) % 2)
            item = jnp.concatenate([acc[i, b, par] for b in range(ZB)], axis=0)
            parts.append(item)
            best = jnp.sum(jnp.where(hit, item, 0.0), axis=0, keepdims=True)
            at = (n // 8) * LANES
            nb_ref[n % 8:n % 8 + 1, at:at + S] = best[:, :S]
            nb2_ref[n % 8:n % 8 + 1, at:at + S] = best[:, S:]
        full = jnp.concatenate(parts, axis=0).T
        for w in range(S // own):
            out_ref[2 * own * w:2 * own * w + own] = full[own * w:own * (w + 1)]
            out_ref[2 * own * w + own:2 * own * (w + 1)] = full[S + own * w:S + own * (w + 1)]

    n = (NP + K) * Z

    def whole(*shape):
        return pl.BlockSpec(shape, lambda i: (0,) * len(shape))

    rows = (NQ + KQ) * ZB * 16
    return pl.pallas_call(
        kernel, grid=(1,),
        out_shape=(jax.ShapeDtypeStruct((N, n), jnp.float32),) + (jax.ShapeDtypeStruct((8, n), jnp.float32),) * 2,
        out_specs=(whole(N, n), whole(8, n), whole(8, n)),
        in_specs=[whole(rows, N), whole(2, LANES, 2 * N), whole(K, Z, LANES),
                  pl.BlockSpec((1, S, LANES), lambda i: (planes - 1, 0, 0)),
                  pl.BlockSpec((1, S, LANES), lambda i: (planes - 1, 0, 1))],
        scratch_shapes=[pltpu.VMEM(((NQ + KQ) * ZB, 16, 2 * LANES), BF)],
        compiler_params=pltpu.CompilerParams(vmem_limit_bytes=60 << 20),
        name="edges")


def factor_solve(N, proj):
    K = len(proj)
    L, inv, y = {}, [], []
    for j in range(K):
        for i in range(j, K):
            v = N[(j, i)]
            for m in range(j):
                v = v - L[(i, m)] * L[(j, m)]
            L[(i, j)] = v
        inv.append(1.0 / jnp.sqrt(L[(j, j)]))
        for i in range(j + 1, K):
            L[(i, j)] = L[(i, j)] * inv[j]
        v = proj[j]
        for m in range(j):
            v = v - L[(j, m)] * y[m]
        y.append(v * inv[j])
    c = [None] * K
    for j in reversed(range(K)):
        v = y[j]
        for i in range(j + 1, K):
            v = v - L[(i, j)] * c[i]
        c[j] = v * inv[j]
    return c


def fit_kernel_for(K, Z):
    pairs = pair_list(K)
    NP = len(pairs)

    def kernel(n_ref, gain_ref):
        n = n_ref[...]
        proj = [n[:, (NP + k) * Z:(NP + k + 1) * Z] for k in range(K)]
        c = factor_solve({kl: n[:, i * Z:(i + 1) * Z] for i, kl in enumerate(pairs)}, proj)
        chi = proj[0] * c[0]
        for k in range(1, K):
            chi = chi + proj[k] * c[k]
        gain_ref[...] = jnp.log1p(chi / K)

    return kernel


def model_kernel_for(K, Z, band):
    pairs = pair_list(K)
    NP = len(pairs)
    half = band // 2
    hp = lax.Precision.HIGHEST

    def kernel(nb_ref, t_ref, x_ref, t2_ref, x2_ref, pack_ref, model_ref):
        S, W = model_ref.shape

        def best(n):
            at = (n // 8) * LANES
            return nb_ref[n % 8:n % 8 + 1, at:at + S]

        c = factor_solve({kl: best(i) for i, kl in enumerate(pairs)}, [best(NP + k) for k in range(K)])
        pad = jnp.zeros((LANES - K, S), jnp.float32)
        coef = jnp.concatenate(c + [pad], axis=0).T
        place = pack_ref[band + 2, :, :1]
        lane = lax.broadcasted_iota(jnp.int32, (S, K * Z), 1)
        cols = jnp.zeros((S, K * Z), jnp.float32)
        for k in range(K):
            cols = jnp.where(lane // Z == k, coef[:, k:k + 1], cols)
        main, edge = None, None
        for part, (a_ref, b_ref) in enumerate(((t_ref, x_ref), (t2_ref, x2_ref))):
            sel = jnp.where((lane % Z + part * Z).astype(jnp.float32) == place, cols, 0.0)
            m = jnp.dot(sel, a_ref[...].reshape(K * Z, W), precision=hp, preferred_element_type=jnp.float32)
            e = jnp.dot(sel, b_ref[...].reshape(K * Z, LANES), precision=hp, preferred_element_type=jnp.float32)
            main = m if main is None else main + m
            edge = e if edge is None else edge + e
        lane = lax.broadcasted_iota(jnp.int32, (S, LANES), 1)
        right = pltpu.roll(edge, LANES - (64 + 2 * half), 1)
        left = pltpu.roll(edge, LANES - half, 1)
        last = jnp.where(lane < half, right, jnp.where(lane >= LANES - half, left, 0.0))
        u = jnp.concatenate([main, last], axis=1)
        wide = W + LANES
        total = None
        for d in range(band):
            shift = (half - d) % wide
            v = (pltpu.roll(u, shift, 1) if shift else u)[:, :W]
            term = pack_ref[d] * v
            total = term if total is None else total + term
        model_ref[...] = total

    return kernel


def body(templates, resolution, coadd_flux, coadd_ivar, best_index, exposures, exposure_mask):
    S, band, W = resolution.shape
    half = band // 2
    zo, K, _ = templates.shape
    nw, ns = lax.axis_size("wave"), lax.axis_size("spec")
    Z = zo * ns // 2
    own = S // nw
    me, wave = lax.axis_index("spec"), lax.axis_index("wave")

    def swap(x, axis, m):
        return lax.ppermute(x, axis, [(i, i ^ m) for i in range(lax.axis_size(axis))])

    def place_for(index):
        rel = (best_index // zo) ^ index
        return ((rel % 2) * Z + (rel // 2) * zo + best_index % zo).astype(jnp.float32)

    where_lane = jnp.arange(W, dtype=jnp.int32)[None, :] < LANES
    plane = jnp.where(where_lane, place_for(me)[:, None], place_for(me ^ 1)[:, None])
    pack = jnp.concatenate([jnp.transpose(resolution, (1, 0, 2)), coadd_ivar[None], coadd_flux[None], plane[None]], axis=0)
    block = jnp.transpose(templates, (1, 0, 2))
    blocks = [block] + [swap(block, "spec", m) for m in range(2, ns, 2)]
    other_pack = swap(pack, "spec", 1)
    ends = jnp.concatenate([block[:, :, W - half:], block[:, :, :half]], axis=2)
    ends = jnp.concatenate([ends] + [swap(ends, "spec", m) for m in range(2, ns, 2)], axis=1)
    up = [(i, i + 1) for i in range(nw - 1)]
    before = lax.ppermute(ends[:, :, :half], "wave", up)
    after = lax.ppermute(ends[:, :, half:], "wave", [(j, i) for i, j in up])
    t = jnp.concatenate(blocks, axis=1)
    acc, aeb = make_main(K, Z, band, S, W)(t, pack, other_pack)
    acc, before, after = lax.optimization_barrier((acc, before, after))
    gap = jnp.zeros((K, Z, 64 - 3 * half), jnp.float32)
    x = jnp.concatenate([before, t[:, :, :2 * half], gap, t[:, :, W - 2 * half:], after, gap], axis=2)
    t2, x2 = swap(t, "spec", 1), swap(x, "spec", 1)
    d, nb, nb2 = make_edge(K, Z, band, S, band + 3, own)(acc, aeb, x, pack, other_pack)
    columns = d.shape[1]
    d = d.reshape(nw, 2 * own, columns)
    bit = 1
    while bit < nw:
        d = d.reshape(d.shape[0] // 2, 2, 2 * own, columns)
        b = (wave // bit) % 2
        keep = lax.dynamic_index_in_dim(d, b, 1, keepdims=False)
        send = lax.dynamic_index_in_dim(d, 1 - b, 1, keepdims=False).reshape(-1, columns)
        if bit == 1:
            d = keep + swap(send, "wave", bit).reshape(keep.shape)
            nb = nb + swap(nb2, "spec", 1)
            nb = nb + swap(nb, "wave", bit)
        else:
            got = swap(jnp.concatenate([send, nb], axis=0), "wave", bit)
            d = keep + got[:-8].reshape(keep.shape)
            nb = nb + got[-8:]
        bit *= 2
    model = pl.pallas_call(
        model_kernel_for(K, Z, band), out_shape=jax.ShapeDtypeStruct((S, W), jnp.float32),
        compiler_params=pltpu.CompilerParams(vmem_limit_bytes=60 << 20), name="model",
    )(nb, t, x, t2, x2, pack)
    rows = lax.all_to_all(model.reshape(nw, own, W), "wave", 0, 0, tiled=True)
    gain = pl.pallas_call(
        fit_kernel_for(K, Z), out_shape=jax.ShapeDtypeStruct((2 * own, Z), jnp.float32), name="fit",
    )(d[0])
    halves = jnp.stack([gain[:own], swap(gain[own:], "spec", 1)], axis=0).reshape(2, own, ns // 2, zo)
    gain = jnp.transpose(halves, (1, 2, 0, 3)).reshape(own, ns, zo)
    bit = 1
    while bit < ns:
        flipped = gain.reshape(own, ns // (2 * bit), 2, bit, zo)[:, :, ::-1].reshape(own, ns, zo)
        gain = jnp.where((me // bit) % 2 == 1, flipped, gain)
        bit *= 2
    gain = gain.reshape(own, ns * zo)
    rows = jnp.transpose(rows, (1, 0, 2)).reshape(own, 1, nw * W)
    residuals = exposure_mask.astype(jnp.float32) * (exposures - rows)
    return gain, residuals


def solution(mesh):
    in_specs = (
        P("spec", None, "wave"),
        P("spec", None, "wave"),
        P("spec", "wave"),
        P("spec", "wave"),
        P("spec"),
        P(("spec", "wave"), None, None),
        P(("spec", "wave"), None, None),
    )
    out_specs = (P(("spec", "wave"), None), P(("spec", "wave"), None, None))
    return jax.shard_map(body, mesh=mesh, in_specs=in_specs, out_specs=out_specs, check_vma=False)
```

```python
import jax
import jax.numpy as jnp
from jax import lax
from jax.experimental import pallas as pl
from jax.experimental.pallas import tpu as pltpu
from jax.sharding import PartitionSpec as P


LANES = 128
BF = jnp.bfloat16


def split(x):
    hi = x.astype(BF)
    return hi, (x - hi.astype(jnp.float32)).astype(BF)


def dot(x, w):
    return jnp.dot(x, w, preferred_element_type=jnp.float32)


def pair_list(K):
    return [(k, l) for k in range(K) for l in range(k, K)]


def put(h_ref, row, lane, width, v):
    hi, lo = split(v)
    h_ref[row:row + 8, lane:lane + v.shape[1]] = hi
    h_ref[row:row + 8, width + lane:width + lane + v.shape[1]] = lo


def pair_block(h_ref, t, s, row, Z, lane, width):
    for i, (k, l) in enumerate(pair_list(len(t))):
        put(h_ref, i * Z + row, lane, width, t[k] * s[l] + t[l] * s[k])


def single_block(h_ref, t, row, Z, lane, width):
    for k in range(len(t)):
        put(h_ref, k * Z + row, lane, width, t[k])


def split_dot(h, w):
    return dot(h, jnp.concatenate([w, w], axis=0))


def place_of(best, me, zo, ns, Z):
    best = best.astype(jnp.int32)
    block = jnp.zeros_like(best)
    for j in range(1, ns):
        block = block + jnp.where(best >= j * zo, 1, 0)
    rel = block ^ me
    return (rel & 1) * Z + (rel >> 1) * zo + best - block * zo


def make_main(K, Z, band, S, W):
    pairs = pair_list(K)
    NP = len(pairs)
    ZB = Z // 8
    half = band // 2
    wide = W + LANES
    top = 24
    N = 2 * S
    step = 16

    def band_matrix(own_ref, other_ref, wb_ref, a_ref, rhs_ref, edge_ref, aeb_ref):
        root_own = jnp.sqrt(own_ref[band])
        root_other = jnp.sqrt(other_ref[band])
        zero = jnp.zeros((band + 1, top, N), jnp.float32)
        wb_ref[:, :top, :] = zero
        wb_ref[:, top + W:, :] = zero
        for d in range(band + 1):
            src = d if d < band else band + 1
            both = jnp.concatenate([own_ref[src] * root_own, other_ref[src] * root_other], axis=0)
            wb_ref[d, top:top + W, :] = both.T

        def block(i, _):
            base = pl.multiple_of(i * step, step)
            for part in range(step // 8):
                acc = [None] * (band + 1)
                for d in range(band):
                    rows = pl.ds(base + (part * 8 + top - step + half - d), 8)
                    v = [wb_ref[e, rows, :] for e in range(d, band + 1)]
                    for e in range(d, band + 1):
                        o = e - d if e < band else band
                        p = v[0] * v[e - d]
                        acc[o] = p if acc[o] is None else acc[o] + p
                acc[0] = acc[0] * 0.5
                for o in range(band + 1):
                    a_ref[o, pl.ds(base + part * 8, 8), :] = acc[o]
            for o in range(band + 1):
                hi, lo = split(a_ref[o, pl.ds(base, step), :])
                rhs_ref[o, pl.ds(base, step), :N] = hi
                rhs_ref[o, pl.ds(base, step), N:] = lo
            return 0

        lax.fori_loop(0, (W + 2 * step) // step, block, 0)
        edge_ref[...] = jnp.zeros_like(edge_ref)
        for o in range(band):
            edge_ref[0, 2 * half * o:2 * half * o + half, :] = a_ref[o, step - half:step, :]
            edge_ref[0, 2 * half * o + half:2 * half * (o + 1), :] = a_ref[o, step + W - o:step + W - o + half, :]
        edge_ref[1, :half, :] = a_ref[band, step - half:step, :]
        edge_ref[1, half:2 * half, :] = a_ref[band, step + W:step + W + half, :]
        for o in range(2):
            hi, lo = split(edge_ref[o])
            aeb_ref[o, :, :N] = hi
            aeb_ref[o, :, N:] = lo

    def kernel(t_ref, own_ref, other_ref, out_ref, aeb_ref,
               wb_ref, a_ref, rhs_ref, edge_ref, s_ref, h0_ref, h1_ref, acc_ref):
        band_matrix(own_ref, other_ref, wb_ref, a_ref, rhs_ref, edge_ref, aeb_ref)
        s_ref[:, :, :W] = t_ref[...]
        s_ref[:, :, W:] = jnp.zeros((K, Z, LANES), jnp.float32)
        acc_ref[...] = jnp.zeros_like(acc_ref)

        G = 2 * LANES

        def build(h_ref):
            for b in range(ZB):
                rows = pl.ds(b * 8, 8)
                for q in range(W // G):
                    t = [t_ref[k, rows, pl.ds(q * G, G)] for k in range(K)]
                    s = [s_ref[k, rows, pl.ds(q * G, G)] for k in range(K)]
                    pair_block(h_ref, t, s, b * 8, Z, q * G, W)

        def advance():
            for k in range(K):
                for b in range(ZB):
                    rows = pl.ds(b * 8, 8)
                    s_ref[k, rows, :] = pltpu.roll(s_ref[k, rows, :], wide - 1, 1)

        def add(h_ref, first, count, w):
            acc_ref[first:first + count] += split_dot(h_ref[:count], w)

        def weights(o):
            return rhs_ref[o, step:step + W, :]

        build(h0_ref)
        advance()

        def pair_step(i, _):
            build(h1_ref)
            advance()
            add(h0_ref, 0, NP * Z, weights(2 * i))
            build(h0_ref)
            advance()
            add(h1_ref, 0, NP * Z, weights(2 * i + 1))
            return 0

        lax.fori_loop(0, band // 2, pair_step, 0)
        for b in range(ZB):
            for q in range(W // G):
                single_block(h1_ref, [t_ref[k, pl.ds(b * 8, 8), pl.ds(q * G, G)] for k in range(K)], b * 8, Z, q * G, W)
        add(h0_ref, 0, NP * Z, weights(band - 1))
        add(h1_ref, NP * Z, K * Z, weights(band))
        out_ref[...] = acc_ref[:, :N] + acc_ref[:, N:]

    return pl.pallas_call(
        kernel,
        out_shape=(jax.ShapeDtypeStruct(((NP + K) * Z, N), jnp.float32),
                   jax.ShapeDtypeStruct((2, LANES, 2 * N), BF)),
        scratch_shapes=[pltpu.VMEM((band + 1, W + 2 * top, N), jnp.float32),
                        pltpu.VMEM((band + 1, W + 2 * step, N), jnp.float32),
                        pltpu.VMEM((band + 1, W + 2 * step, 2 * N), BF),
                        pltpu.VMEM((2, LANES, N), jnp.float32),
                        pltpu.VMEM((K, Z, wide), jnp.float32),
                        pltpu.VMEM((NP * Z, 2 * W), BF),
                        pltpu.VMEM((NP * Z, 2 * W), BF),
                        pltpu.VMEM(((NP + K) * Z, 2 * N), jnp.float32)],
        compiler_params=pltpu.CompilerParams(vmem_limit_bytes=60 << 20),
        name="normals")


def make_edge(K, Z, band, S, own, ns):
    NP = K * (K + 1) // 2
    ZB = Z // 8
    half = band // 2
    N = 2 * S

    def kernel(acc_ref, aeb_ref, x_ref, own_ref, other_ref, me_ref, left_ref, right_ref, nb_ref, nb2_ref, h_ref):
        inp = lax.broadcasted_iota(jnp.int32, (LANES, LANES), 0)
        outp = lax.broadcasted_iota(jnp.int32, (LANES, LANES), 1)
        dd = outp // (2 * half)
        ii = outp % (2 * half)
        isl = ii < half
        valid = outp < 2 * half * band
        src1 = jnp.where(isl, ii, 64 + half + ii)
        src2 = jnp.where(isl, ii + dd, 64 + half + ii - dd)
        sel1 = ((inp == src1) & valid).astype(jnp.float32).astype(BF)
        sel2 = ((inp == src2) & valid).astype(jnp.float32).astype(BF)
        x = x_ref[...].reshape(K * Z, LANES)
        hi = x.astype(BF)
        rest = x - hi.astype(jnp.float32)
        mid, low = split(rest)
        picks = jnp.concatenate([sel1, sel2], axis=1)
        e = (dot(hi, picks) + dot(mid, picks)) + dot(low, picks)
        e1 = e[:, :LANES].reshape(K, Z, LANES)
        e2 = e[:, LANES:].reshape(K, Z, LANES)
        for b in range(ZB):
            t = [e1[k, b * 8:(b + 1) * 8] for k in range(K)]
            s = [e2[k, b * 8:(b + 1) * 8] for k in range(K)]
            pair_block(h_ref, t, s, b * 8, Z, 0, LANES)
            single_block(h_ref.at[NP * Z:], t, b * 8, Z, 0, LANES)
        sums = []
        for part, o in ((h_ref[:NP * Z], 0), (h_ref[NP * Z:], 1)):
            v = split_dot(part, aeb_ref[o])
            sums.append(v[:, :N] + v[:, N:])
        acc = acc_ref[...] + jnp.concatenate(sums, axis=0)
        best = jnp.concatenate([own_ref[...], other_ref[...]], axis=1)
        hit = lax.broadcasted_iota(jnp.int32, (Z, N), 0) == place_of(best, me_ref[...], Z * 2 // ns, ns, Z)
        nb_ref[...] = jnp.zeros_like(nb_ref)
        nb2_ref[...] = jnp.zeros_like(nb2_ref)
        for n in range(NP + K):
            item = acc[n * Z:(n + 1) * Z]
            best = jnp.sum(jnp.where(hit, item, 0.0), axis=0, keepdims=True)
            row, at = n % R, (n // R) * LANES
            nb_ref[row:row + 1, at:at + S] = best[:, :S]
            nb2_ref[row:row + 1, at:at + S] = best[:, S:]
        full = acc.T
        for w in range(S // own):
            block = jnp.concatenate([full[own * w:own * (w + 1)], full[S + own * w:S + own * (w + 1)]], axis=0)
            left_ref[R * w:R * (w + 1)] = block[:, :cut]
            right_ref[R * w:R * (w + 1)] = block[:, cut:]

    n = (NP + K) * Z
    R = 2 * own
    cut = -(-n // (2 * LANES)) * LANES
    width = -(-(NP + K) // R) * LANES

    def whole(*shape):
        return pl.BlockSpec(shape, lambda i: (0,) * len(shape))

    rows = (NP + K) * Z
    return pl.pallas_call(
        kernel, grid=(1,),
        out_shape=tuple(jax.ShapeDtypeStruct(shape, jnp.float32) for shape in ((N, cut), (N, n - cut), (R, width), (R, width))),
        out_specs=(whole(N, cut), whole(N, n - cut), whole(R, width), whole(R, width)),
        in_specs=[whole(rows, N), whole(2, LANES, 2 * N), whole(K, Z, LANES),
                  whole(1, S), whole(1, S), whole(1, 1)],
        scratch_shapes=[pltpu.VMEM(((NP + K) * Z, 2 * LANES), BF)],
        compiler_params=pltpu.CompilerParams(vmem_limit_bytes=60 << 20),
        name="edges")


def factor_solve(N, proj):
    K = len(proj)
    L, inv, y = {}, [], []
    for j in range(K):
        for i in range(j, K):
            v = N[(j, i)]
            for m in range(j):
                v = v - L[(i, m)] * L[(j, m)]
            L[(i, j)] = v
        inv.append(1.0 / jnp.sqrt(L[(j, j)]))
        for i in range(j + 1, K):
            L[(i, j)] = L[(i, j)] * inv[j]
        v = proj[j]
        for m in range(j):
            v = v - L[(j, m)] * y[m]
        y.append(v * inv[j])
    c = [None] * K
    for j in reversed(range(K)):
        v = y[j]
        for i in range(j + 1, K):
            v = v - L[(i, j)] * c[i]
        c[j] = v * inv[j]
    return c


def fit_kernel_for(K, Z):
    pairs = pair_list(K)
    NP = len(pairs)

    def kernel(n_ref, gain_ref):
        n = n_ref[...].T
        proj = [n[(NP + k) * Z:(NP + k + 1) * Z] for k in range(K)]
        c = factor_solve({kl: n[i * Z:(i + 1) * Z] for i, kl in enumerate(pairs)}, proj)
        chi = proj[0] * c[0]
        for k in range(1, K):
            chi = chi + proj[k] * c[k]
        gain_ref[...] = jnp.log1p(chi / K).T

    return kernel


def model_kernel_for(K, Z, band, ns):
    pairs = pair_list(K)
    NP = len(pairs)
    half = band // 2
    hp = lax.Precision.HIGHEST

    def kernel(nb_ref, t_ref, x_ref, t2_ref, x2_ref, pack_ref, best_ref, me_ref, model_ref):
        S, W = model_ref.shape

        def best(n):
            rows = nb_ref.shape[0]
            at = (n // rows) * LANES
            return nb_ref[n % rows:n % rows + 1, at:at + S]

        c = factor_solve({kl: best(i) for i, kl in enumerate(pairs)}, [best(NP + k) for k in range(K)])
        pad = jnp.zeros((LANES - K, S), jnp.float32)
        coef = jnp.concatenate(c + [pad], axis=0).T
        place = place_of(jnp.broadcast_to(best_ref[...].astype(jnp.float32), (S, S)).T[:, :1], me_ref[...], Z * 2 // ns, ns, Z)
        lane = lax.broadcasted_iota(jnp.int32, (S, K * Z), 1)
        cols = jnp.zeros((S, K * Z), jnp.float32)
        for k in range(K):
            cols = jnp.where(lane // Z == k, coef[:, k:k + 1], cols)
        main, edge = None, None
        for part, (a_ref, b_ref) in enumerate(((t_ref, x_ref), (t2_ref, x2_ref))):
            sel = jnp.where(lane % Z + part * Z == place, cols, 0.0)
            m = jnp.dot(sel, a_ref[...].reshape(K * Z, W), precision=hp, preferred_element_type=jnp.float32)
            e = jnp.dot(sel, b_ref[...].reshape(K * Z, LANES), precision=hp, preferred_element_type=jnp.float32)
            main = m if main is None else main + m
            edge = e if edge is None else edge + e
        lane = lax.broadcasted_iota(jnp.int32, (S, LANES), 1)
        right = pltpu.roll(edge, LANES - (64 + 2 * half), 1)
        left = pltpu.roll(edge, LANES - half, 1)
        last = jnp.where(lane < half, right, jnp.where(lane >= LANES - half, left, 0.0))
        u = jnp.concatenate([main, last], axis=1)
        wide = W + LANES
        total = None
        for d in range(band):
            shift = (half - d) % wide
            v = (pltpu.roll(u, shift, 1) if shift else u)[:, :W]
            term = pack_ref[d] * v
            total = term if total is None else total + term
        model_ref[...] = total

    return kernel


def body(templates, resolution, coadd_flux, coadd_ivar, best_index, exposures, exposure_mask):
    S, band, W = resolution.shape
    half = band // 2
    zo, K, _ = templates.shape
    nw, ns = lax.axis_size("wave"), lax.axis_size("spec")
    Z = zo * ns // 2
    own = S // nw
    me, wave = lax.axis_index("spec"), lax.axis_index("wave")

    def swap(x, axis, m):
        return lax.ppermute(x, axis, [(i, i ^ m) for i in range(lax.axis_size(axis))])

    ys = range(2, ns, 2)
    block = jnp.transpose(templates, (1, 0, 2))
    flat = block.reshape(K * zo, W)
    others = [swap(flat, "spec", m).reshape(K, zo, W) for m in ys]
    ends = jnp.concatenate([templates[:, :, W - half:], templates[:, :, :half]], axis=2)
    ends = jnp.transpose(ends, (2, 0, 1)).reshape(2 * half, zo * K)
    ends = jnp.concatenate([ends] + [swap(ends, "spec", m) for m in ys], axis=1)
    before = lax.ppermute(ends[:half], "wave", [(i, i + 1) for i in range(nw - 1)])
    after = lax.ppermute(ends[half:], "wave", [(i + 1, i) for i in range(nw - 1)])
    pack = jnp.concatenate([jnp.transpose(resolution, (1, 0, 2)), coadd_ivar[None], coadd_flux[None]], axis=0)
    other_pack = swap(pack, "spec", 1)
    wanted = best_index.reshape(1, S)
    other_wanted = swap(wanted, "spec", 1)
    t = jnp.concatenate([block] + others, axis=1)
    index = jnp.full((1, 1), me, jnp.int32)
    acc, aeb = make_main(K, Z, band, S, W)(t, pack, other_pack)
    acc, before, after = lax.optimization_barrier((acc, before, after))
    gap = jnp.zeros((K, Z, 64 - 3 * half), jnp.float32)
    before, after = (jnp.transpose(v.reshape(half, Z, K), (2, 1, 0)) for v in (before, after))
    x = jnp.concatenate([before, t[:, :, :2 * half], gap, t[:, :, W - 2 * half:], after, gap], axis=2)
    t2, x2 = swap(t, "spec", 1), swap(x, "spec", 1)
    left, right, nb, nb2 = make_edge(K, Z, band, S, own, ns)(acc, aeb, x, wanted, other_wanted, index)

    R = 2 * own

    def halve(d, bit, order, extra=None):
        axis = order.index(bit)
        b = (wave // bit) % 2
        columns = d.shape[-1]
        keep = lax.dynamic_index_in_dim(d, b, axis, keepdims=False)
        send = lax.dynamic_index_in_dim(d, 1 - b, axis, keepdims=False).reshape(-1, columns)
        rows = send.shape[0]
        if extra is not None:
            send = jnp.concatenate([send, jnp.tile(extra, (rows // R, 1))], axis=1)
        got = swap(send, "wave", bit)
        if extra is not None:
            extra = extra + got[:R, columns:]
        d = keep + got[:rows, :columns].reshape(keep.shape)
        return d, order[:axis] + order[axis + 1:], extra

    bits = [1 << i for i in range(nw.bit_length() - 1)]
    order = bits[::-1]
    left, right = (v.reshape([2] * len(bits) + [R, v.shape[1]]) for v in (left, right))
    left, order_a, _ = halve(left, bits[0], order)
    right, order_b, _ = halve(right, bits[1], order)
    nb = nb + swap(nb2, "spec", 1)
    got = swap(nb, "wave", bits[0])
    left, order_a, _ = halve(left, bits[1], order_a)
    right, order_b, _ = halve(right, bits[0], order_b)
    nb = nb + got
    nb = nb + swap(nb, "wave", bits[1])
    d = jnp.concatenate([left, right], axis=-1)
    for bit in bits[2:]:
        d, order_a, nb = halve(d, bit, order_a, nb)
    model = pl.pallas_call(
        model_kernel_for(K, Z, band, ns), out_shape=jax.ShapeDtypeStruct((S, W), jnp.float32),
        compiler_params=pltpu.CompilerParams(vmem_limit_bytes=60 << 20), name="model",
    )(nb, t, x, t2, x2, pack, wanted, index)
    rows = lax.all_to_all(model.reshape(nw, own, W), "wave", 0, 0, tiled=True)
    gain = pl.pallas_call(
        fit_kernel_for(K, Z), out_shape=jax.ShapeDtypeStruct((2 * own, Z), jnp.float32), name="fit",
    )(d)
    halves = jnp.stack([gain[:own], swap(gain[own:], "spec", 1)], axis=0).reshape(2, own, ns // 2, zo)
    gain = jnp.transpose(halves, (1, 2, 0, 3)).reshape(own, ns, zo)
    bit = 1
    while bit < ns:
        flipped = gain.reshape(own, ns // (2 * bit), 2, bit, zo)[:, :, ::-1].reshape(own, ns, zo)
        gain = jnp.where((me // bit) % 2 == 1, flipped, gain)
        bit *= 2
    gain = gain.reshape(own, ns * zo)
    rows = jnp.transpose(rows, (1, 0, 2)).reshape(own, 1, nw * W)
    residuals = exposure_mask.astype(jnp.float32) * (exposures - rows)
    return gain, residuals


def solution(mesh):
    in_specs = (
        P("spec", None, "wave"),
        P("spec", None, "wave"),
        P("spec", "wave"),
        P("spec", "wave"),
        P("spec"),
        P(("spec", "wave"), None, None),
        P(("spec", "wave"), None, None),
    )
    out_specs = (P(("spec", "wave"), None), P(("spec", "wave"), None, None))

    return jax.shard_map(body, mesh=mesh, in_specs=in_specs, out_specs=out_specs, check_vma=False)
```
